32 devices in a mesh: dp: 8 (over y, x, core), ctx: 4 (over z).
Axes of the slice: x: 2, y: 2, z: 4, core: 2. Of those that a mesh axis runs over, the one named last changes fastest.
Arguments:
- tokens: bfloat16 [8, 512, 1088], P('dp', 'ctx'), may hold values from -32 to 32
- cotangent: bfloat16 [8, 512, 1088], P('dp', 'ctx'), may hold values from -6 to 6
- ln1_gain: float32 [1088], P('dp'), may hold values from 0.5 to 1.5
- ln1_bias: float32 [1088], P('dp'), may hold values from -1.5 to 1.5
- qkv_weight: bfloat16 [1088, 3264], P('dp'), may hold values from -10 to 10
- qv_bias: float32 [2, 1088], P(None, 'dp'), may hold values from -1.5 to 1.5
- out_weight: bfloat16 [1088, 1088], P('dp'), may hold values from -1.5 to 1.5
- out_bias: float32 [1088], P('dp'), may hold values from -1.5 to 1.5
- ln2_gain: float32 [1088], P('dp'), may hold values from 0.5 to 1.5
- ln2_bias: float32 [1088], P('dp'), may hold values from -1.5 to 1.5
- up_weight: bfloat16 [1088, 4352], P('dp'), may hold values from -0.1875 to 0.1875
- up_bias: float32 [4352], P('dp'), may hold values from -1.5 to 1.5
- down_weight: bfloat16 [4352, 1088], P('dp'), may hold values from -0.09375 to 0.09375
- down_bias: float32 [1088], P('dp'), may hold values from -1.5 to 1.5
Outputs:
- activations: bfloat16 [8, 512, 1088], P('dp', 'ctx')
- input_grad: bfloat16 [8, 512, 1088], P('dp', 'ctx')
- ln1_gain_grad: float32 [1088], P('dp')
- ln1_bias_grad: float32 [1088], P('dp')
- qkv_grad: float32 [1088, 3264], P('dp')
- qv_bias_grad: float32 [2, 1088], P(None, 'dp')
- out_grad: float32 [1088, 1088], P('dp')
- out_bias_grad: float32 [1088], P('dp')
- ln2_gain_grad: float32 [1088], P('dp')
- ln2_bias_grad: float32 [1088], P('dp')
- up_grad: float32 [1088, 4352], P('dp')
- up_bias_grad: float32 [4352], P('dp')
- down_grad: float32 [4352, 1088], P('dp')
- down_bias_grad: float32 [1088], P('dp')
The draws below stay inside these ranges and needn't reach their ends.
All inputs are finite; a program needn't handle non-finite values.
Results may differ from the reference program's by a relative error of at most 0.012.
Values may be sent and summed in bfloat16 or wider, within the bound.
A program may use at most 192 MiB of HBM per device.

```python
import math
import jax
import jax.numpy as jnp
from jax import lax

D = 1088
H = 17
HD = 64
FF = 4352
SEQ = 512
NSEQ = 8


def draw_tokens(key, part):
    first_key, second_key, third_key = jax.random.split(key, 3)
    column_scale = jnp.exp(jax.random.uniform(third_key, (1, 1, D), minval=math.log(0.3), maxval=math.log(3.0)))
    row_scale = jnp.exp(jax.random.uniform(second_key, (NSEQ, SEQ, 1), minval=math.log(0.3), maxval=math.log(3.0)))
    result = jax.random.normal(first_key, (NSEQ, SEQ, D)) * row_scale * column_scale
    return jnp.clip(result, -32.0, 32.0).astype(jnp.bfloat16)


def draw_qkv_weight(key, part):
    first_key = jax.random.fold_in(key, 0)
    scale = D ** (-0.5)
    result = jax.random.normal(first_key, (D, 3 * D)) * scale
    return jnp.clip(result, -10.0, 10.0).astype(jnp.bfloat16)


def steps_of(own_key, dims, pieces, least, largest):
    gain = 1.0
    for dim, shards_of in pieces:
        steps = jax.random.uniform(jax.random.fold_in(jax.random.fold_in(own_key, 6), dim), (shards_of,), jnp.float32, least / len(pieces), largest / len(pieces))
        gain = gain * jnp.repeat(jnp.exp(steps), dims[dim] // shards_of).reshape((-1,) + (1,) * (len(dims) - 1 - dim))
    return gain


def scatter_about(own_key, extent, spread, most, cuts=(), dtype=jnp.bfloat16):
    gain = steps_of(own_key, extent, cuts, -0.22, 0.18) if cuts else 1.0
    values = jax.random.normal(own_key, extent, jnp.float32) * spread * gain
    return jnp.minimum(jnp.maximum(values, -most), most).astype(dtype)


def setup_inputs(seed: int = 0) -> dict:
    key_list = jax.random.split(jax.random.key(seed), 15)
    return {
        "tokens": draw_tokens(jax.random.fold_in(key_list[14], 71), 0),
        "cotangent": scatter_about(key_list[1], (NSEQ, SEQ, D), 1.0, 6.0, ((0, 8), (1, 4))),
        "ln1_gain": jnp.clip(1.0 + 0.1 * jax.random.normal(key_list[2], (D,), jnp.float32), 0.5, 1.5),
        "ln1_bias": scatter_about(key_list[3], (D,), 0.3, 1.5, ((0, 8),), jnp.float32),
        "qkv_weight": draw_qkv_weight(jax.random.fold_in(key_list[14], 71), 0),
        "qv_bias": scatter_about(key_list[5], (2, D), 0.3, 1.5, ((1, 8),), jnp.float32),
        "out_weight": scatter_about(key_list[6], (D, D), (max(1, 8 * D // SEQ)) ** -0.5, 1.5, ((0, 8),)),
        "out_bias": scatter_about(key_list[7], (D,), 0.3, 1.5, ((0, 8),), jnp.float32),
        "ln2_gain": jnp.clip(1.0 + 0.1 * jax.random.normal(key_list[8], (D,), jnp.float32), 0.5, 1.5),
        "ln2_bias": scatter_about(key_list[9], (D,), 0.3, 1.5, ((0, 8),), jnp.float32),
        "up_weight": scatter_about(key_list[10], (D, FF), D ** -0.5, 0.1875, ((0, 8),)),
        "up_bias": scatter_about(key_list[11], (FF,), 0.3, 1.5, ((0, 8),), jnp.float32),
        "down_weight": scatter_about(key_list[12], (FF, D), FF ** -0.5, 0.09375, ((0, 8),)),
        "down_bias": scatter_about(key_list[13], (D,), 0.3, 1.5, ((0, 8),), jnp.float32),
    }


EPSILON = 1e-05
ROOT_HALF = 0.7071067811865476
INV_ROOT_TAU = 0.3989422804014327

def rounded(values):
    return lax.optimization_barrier(values.astype(jnp.bfloat16))

def norm_parts(values, norm_gain, norm_shift):
    average = lax.optimization_barrier(jnp.mean(values, axis=-1, keepdims=True))
    centered = values - average
    inverse = lax.rsqrt(lax.optimization_barrier(jnp.mean(centered * centered, axis=-1, keepdims=True)) + EPSILON)
    normed = centered * inverse
    return (normed, inverse, normed * norm_gain + norm_shift)

def norm_back(grad_out, normed, inverse, norm_gain):
    scaled = grad_out * norm_gain
    return inverse * (scaled - lax.optimization_barrier(jnp.mean(scaled, axis=-1, keepdims=True)) - normed * lax.optimization_barrier(jnp.mean(scaled * normed, axis=-1, keepdims=True)))

def gelu_exact(pre_act):
    return 0.5 * pre_act * (1.0 + lax.erf(pre_act * ROOT_HALF))

def gelu_slope(pre_act):
    return 0.5 * (1.0 + lax.erf(pre_act * ROOT_HALF)) + pre_act * jnp.exp(-0.5 * pre_act * pre_act) * INV_ROOT_TAU

def heads_first(matrix):
    return matrix.reshape(matrix.shape[0], H, HD).transpose(1, 0, 2)

def heads_last(stacked):
    return stacked.transpose(1, 0, 2).reshape(stacked.shape[1], H * HD)

def sequence_pass(params, seq_tokens, seq_cot):
    ln1_gain, ln1_bias, qkv_weight, qv_bias, out_weight, out_bias, ln2_gain, ln2_bias, up_weight, up_bias, down_weight, down_bias = params
    scale = float(HD) ** (-0.5)
    length = seq_tokens.shape[0]
    inputs_full = seq_tokens.astype(jnp.float32)
    normed_one, inverse_one, pre_one = norm_parts(inputs_full, ln1_gain, ln1_bias)
    act_one = rounded(pre_one)
    mixed_qkv = jnp.dot(act_one, qkv_weight, preferred_element_type=jnp.float32)
    queries = rounded(mixed_qkv[:, :D] + qv_bias[0])
    keys_low = rounded(mixed_qkv[:, D:2 * D])
    values_low = rounded(mixed_qkv[:, 2 * D:] + qv_bias[1])
    query_heads = heads_first(queries).astype(jnp.float32)
    key_heads = heads_first(keys_low).astype(jnp.float32)
    value_heads = heads_first(values_low).astype(jnp.float32)
    scores = jnp.einsum('hqd,hkd->hqk', query_heads, key_heads) * scale
    positions = jnp.arange(length)
    allowed = positions[None, :] <= positions[:, None]
    scores = jnp.where(allowed, scores, -1e+30)
    highest = lax.optimization_barrier(jnp.max(scores, axis=-1, keepdims=True))
    summed = lax.optimization_barrier(jnp.sum(jnp.where(allowed, jnp.exp(scores - highest), 0.0), axis=-1, keepdims=True))
    log_total = highest + jnp.log(summed)
    probs_full = jnp.where(allowed, jnp.exp(scores - log_total), 0.0)
    probs_low = rounded(probs_full).astype(jnp.float32)
    attended = rounded(heads_last(jnp.einsum('hqk,hkd->hqd', probs_low, value_heads)))
    hidden_one = inputs_full + (jnp.dot(attended, out_weight, preferred_element_type=jnp.float32) + out_bias)
    normed_two, inverse_two, pre_two = norm_parts(hidden_one, ln2_gain, ln2_bias)
    act_two = rounded(pre_two)
    pre_up = jnp.dot(act_two, up_weight, preferred_element_type=jnp.float32) + up_bias
    activated = rounded(gelu_exact(pre_up))
    output_full = hidden_one + (jnp.dot(activated, down_weight, preferred_element_type=jnp.float32) + down_bias)
    cot_full = seq_cot.astype(jnp.float32)
    down_bias_grad = lax.optimization_barrier(jnp.sum(cot_full, axis=0))
    down_grad = jnp.dot(activated.T, seq_cot, preferred_element_type=jnp.float32)
    dpre = jnp.dot(seq_cot, down_weight.T, preferred_element_type=jnp.float32) * gelu_slope(pre_up)
    up_bias_grad = lax.optimization_barrier(jnp.sum(dpre, axis=0))
    dpre_low = rounded(dpre)
    up_grad = jnp.dot(act_two.T, dpre_low, preferred_element_type=jnp.float32)
    dnorm_two = jnp.dot(dpre_low, up_weight.T, preferred_element_type=jnp.float32)
    ln2_gain_grad = lax.optimization_barrier(jnp.sum(dnorm_two * normed_two, axis=0))
    ln2_bias_grad = lax.optimization_barrier(jnp.sum(dnorm_two, axis=0))
    dhidden = cot_full + norm_back(dnorm_two, normed_two, inverse_two, ln2_gain)
    out_bias_grad = lax.optimization_barrier(jnp.sum(dhidden, axis=0))
    dhidden_low = rounded(dhidden)
    out_grad = jnp.dot(attended.T, dhidden_low, preferred_element_type=jnp.float32)
    dattended = rounded(jnp.dot(dhidden_low, out_weight.T, preferred_element_type=jnp.float32))
    dout_heads = heads_first(dattended).astype(jnp.float32)
    delta = lax.optimization_barrier(jnp.sum(dout_heads * heads_first(attended).astype(jnp.float32), axis=-1, keepdims=True))
    dprobs = jnp.einsum('hqd,hkd->hqk', dout_heads, value_heads)
    dscores = rounded(probs_full * (dprobs - delta)).astype(jnp.float32)
    dqueries = heads_last(jnp.einsum('hqk,hkd->hqd', dscores, key_heads) * scale)
    dkeys = heads_last(jnp.einsum('hqk,hqd->hkd', dscores, query_heads) * scale)
    dvalues = heads_last(jnp.einsum('hqk,hqd->hkd', probs_low, dout_heads))
    qv_bias_grad = jnp.stack([lax.optimization_barrier(jnp.sum(dqueries, axis=0)), lax.optimization_barrier(jnp.sum(dvalues, axis=0))])
    dqkv = rounded(jnp.concatenate([dqueries, dkeys, dvalues], axis=1))
    qkv_grad = jnp.dot(act_one.T, dqkv, preferred_element_type=jnp.float32)
    dnorm_one = jnp.dot(dqkv, qkv_weight.T, preferred_element_type=jnp.float32)
    ln1_gain_grad = lax.optimization_barrier(jnp.sum(dnorm_one * normed_one, axis=0))
    ln1_bias_grad = lax.optimization_barrier(jnp.sum(dnorm_one, axis=0))
    input_grad = (dhidden + norm_back(dnorm_one, normed_one, inverse_one, ln1_gain)).astype(jnp.bfloat16)
    grads = (ln1_gain_grad, ln1_bias_grad, qkv_grad, qv_bias_grad, out_grad, out_bias_grad, ln2_gain_grad, ln2_bias_grad, up_grad, up_bias_grad, down_grad, down_bias_grad)
    return (output_full.astype(jnp.bfloat16), input_grad, grads)

def reference(tokens, cotangent, ln1_gain, ln1_bias, qkv_weight, qv_bias, out_weight, out_bias, ln2_gain, ln2_bias, up_weight, up_bias, down_weight, down_bias):
    params = (ln1_gain, ln1_bias, qkv_weight, qv_bias, out_weight, out_bias, ln2_gain, ln2_bias, up_weight, up_bias, down_weight, down_bias)
    starting = jax.tree.map(lambda element: jnp.zeros(element.shape, jnp.float32), params)

    def scan_step(running, sequence_pair):
        output_seq, grad_seq, grads = sequence_pass(params, sequence_pair[0], sequence_pair[1])
        running = jax.tree.map(lambda before, update: before + update, running, grads)
        return (running, (output_seq, grad_seq))
    totals, (outputs_all, grads_all) = lax.scan(scan_step, starting, (tokens, cotangent))
    return (outputs_all, grads_all, totals[0], totals[1], totals[2], totals[3], totals[4], totals[5], totals[6], totals[7], totals[8], totals[9], totals[10], totals[11])
```

```python
import jax
import jax.numpy as jnp
from jax import lax
from jax.experimental import pallas as pl
from jax.experimental.pallas import tpu as pltpu
from jax.sharding import PartitionSpec as P

D = 1088
H = 17
HD = 64
EVEN = H // 2 * 2 * HD


EPSILON = 1e-05
ROOT_HALF = 0.7071067811865476
INV_ROOT_TAU = 0.3989422804014327

F32 = jnp.float32
LOW = jnp.bfloat16

def norm_parts(values, norm_gain, norm_shift):
    average = jnp.mean(values, axis=-1, keepdims=True)
    centered = values - average
    inverse = lax.rsqrt(jnp.mean(centered * centered, axis=-1, keepdims=True) + EPSILON)
    normed = centered * inverse
    return (normed, inverse, normed * norm_gain + norm_shift)


def norm_back(grad_out, normed, inverse, norm_gain):
    scaled = grad_out * norm_gain
    return inverse * (
        scaled
        - jnp.mean(scaled, axis=-1, keepdims=True)
        - normed * jnp.mean(scaled * normed, axis=-1, keepdims=True)
    )


def gelu_exact(pre_act):
    return 0.5 * pre_act * (1.0 + lax.erf(pre_act * ROOT_HALF))


def gelu_slope(pre_act):
    return (
        0.5 * (1.0 + lax.erf(pre_act * ROOT_HALF))
        + pre_act * jnp.exp(-0.5 * pre_act * pre_act) * INV_ROOT_TAU
    )


def dot(left, right, left_dim, right_dim):
    return lax.dot_general(
        left, right, (((left_dim,), (right_dim,)), ((), ())), preferred_element_type=F32
    )


def gather(block):
    return lax.all_gather(block, "dp", axis=0, tiled=True)


def allowed_pairs(rows, columns):
    first = lax.axis_index("ctx") * rows
    query_pos = first + lax.broadcasted_iota(jnp.int32, (rows, columns), 0)
    key_pos = lax.broadcasted_iota(jnp.int32, (rows, columns), 1)
    return key_pos <= query_pos


def pack_pairs(keys, values):
    return jnp.concatenate(
        [keys[:, :EVEN], values[:, :EVEN], keys[:, EVEN:], values[:, EVEN:]], axis=1
    )


def unpack_pairs(packed):
    return jnp.concatenate(
        [
            packed[:, :EVEN],
            packed[:, 2 * EVEN : 2 * EVEN + HD],
            packed[:, EVEN : 2 * EVEN],
            packed[:, 2 * EVEN + HD :],
        ],
        axis=1,
    )


def over_heads(one_group):
    def step(pair, carry):
        first = pl.multiple_of(pair * 2 * HD, 2 * HD)
        later = pl.multiple_of(EVEN + pair * 2 * HD, 2 * HD)
        one_group(2 * pair, 2, pl.ds(first, 2 * HD), pl.ds(later, 2 * HD))
        return carry

    lax.fori_loop(0, H // 2, step, 0)
    one_group(H - 1, 1, None, None)


def views(head, count, cols, value_cols):
    if count == 2:
        return cols, cols, value_cols
    return slice(EVEN, D), slice(2 * EVEN, 2 * EVEN + HD), slice(2 * EVEN + HD, 2 * D)


def attend_kernel(q_ref, kv_ref, out_ref, log_ref):
    rows, columns = q_ref.shape[0], kv_ref.shape[0]
    allowed = allowed_pairs(rows, columns)
    scale = float(HD) ** (-0.5)
    lane = lax.broadcasted_iota(jnp.int32, (rows, 128), 1)
    log_ref[...] = jnp.zeros((rows, 128), F32)

    def one_group(head, count, cols, value_cols):
        q_cols, k_cols, v_cols = views(head, count, cols, value_cols)
        queries, keys, values = q_ref[:, q_cols], kv_ref[:, k_cols], kv_ref[:, v_cols]
        mixed = []
        logs = log_ref[...]
        for half in range(count):
            own = slice(half * HD, (half + 1) * HD)
            scores = jnp.where(
                allowed, dot(queries[:, own], keys[:, own], 1, 1) * scale, -1e30
            )
            highest = jnp.max(scores, axis=1, keepdims=True)
            powers = jnp.exp(scores - highest)
            summed = jnp.sum(powers, axis=1, keepdims=True)
            probs_low = (powers * (1.0 / summed)).astype(LOW)
            mixed.append(dot(probs_low, values[:, own], 1, 0).astype(LOW))
            logs = jnp.where(lane == head + half, highest + jnp.log(summed), logs)
        log_ref[...] = logs
        out_ref[:, q_cols] = jnp.concatenate(mixed, axis=1) if count == 2 else mixed[0]

    over_heads(one_group)


def attend_back_kernel(q_ref, kv_ref, out_ref, dout_ref, log_ref, dq_ref, dkv_ref, sum_ref):
    rows, columns = q_ref.shape[0], kv_ref.shape[0]
    allowed = allowed_pairs(rows, columns)
    scale = float(HD) ** (-0.5)
    lane = lax.broadcasted_iota(jnp.int32, (rows, 128), 1)

    def one_group(head, count, cols, value_cols):
        q_cols, k_cols, v_cols = views(head, count, cols, value_cols)
        queries, keys, values = q_ref[:, q_cols], kv_ref[:, k_cols], kv_ref[:, v_cols]
        douts, outs, logs = dout_ref[:, q_cols], out_ref[:, q_cols], log_ref[...]
        grads = []
        for half in range(count):
            own = slice(half * HD, (half + 1) * HD)
            query, key, dout = queries[:, own], keys[:, own], douts[:, own]
            log_total = jnp.sum(jnp.where(lane == head + half, logs, 0.0), axis=1, keepdims=True)
            scores = jnp.where(allowed, dot(query, key, 1, 1) * scale, -1e30)
            probs = jnp.exp(scores - log_total)
            delta = jnp.sum(dout.astype(F32) * outs[:, own].astype(F32), axis=1, keepdims=True)
            dscores = (probs * (dot(dout, values[:, own], 1, 1) - delta)).astype(LOW)
            grads.append(
                (
                    dot(dscores, key, 1, 0) * scale,
                    dot(dscores, query, 0, 0) * scale,
                    dot(probs.astype(LOW), dout, 0, 0),
                )
            )
        dquery, dkey, dvalue = [
            jnp.concatenate(terms, axis=1) if count == 2 else terms[0] for terms in zip(*grads)
        ]
        dq_ref[:, q_cols] = dquery.astype(LOW)
        dkv_ref[:, k_cols] = dkey.astype(LOW)
        dkv_ref[:, v_cols] = dvalue.astype(LOW)
        sum_ref[0:1, q_cols] = jnp.sum(dquery, axis=0, keepdims=True)
        sum_ref[1:2, q_cols] = jnp.sum(dvalue, axis=0, keepdims=True)

    over_heads(one_group)


def attend(queries, key_values):
    rows, columns = queries.shape[0], key_values.shape[0]
    return pl.pallas_call(
        attend_kernel,
        out_shape=(
            jax.ShapeDtypeStruct((rows, D), LOW),
            jax.ShapeDtypeStruct((rows, 128), F32),
        ),
        cost_estimate=pl.CostEstimate(
            flops=4 * rows * columns * D,
            bytes_accessed=4 * rows * D + 4 * columns * D,
            transcendentals=H * rows * columns,
        ),
        name="attend",
    )(queries, key_values)


def attend_back(queries, key_values, attended, dattended, logs):
    rows, columns = queries.shape[0], key_values.shape[0]
    return pl.pallas_call(
        attend_back_kernel,
        out_shape=(
            jax.ShapeDtypeStruct((rows, D), LOW),
            jax.ShapeDtypeStruct((columns, 2 * D), LOW),
            jax.ShapeDtypeStruct((2, D), F32),
        ),
        cost_estimate=pl.CostEstimate(
            flops=10 * rows * columns * D,
            bytes_accessed=10 * rows * D + 8 * columns * D,
            transcendentals=H * rows * columns,
        ),
        name="attend_back",
    )(queries, key_values, attended, dattended, logs)


def per_device(
    tokens,
    cotangent,
    ln1_gain,
    ln1_bias,
    qkv_weight,
    qv_bias,
    out_weight,
    out_bias,
    ln2_gain,
    ln2_bias,
    up_weight,
    up_bias,
    down_weight,
    down_bias,
):
    shards = lax.axis_size("dp")
    part = D // shards
    vectors = jnp.concatenate(
        [
            ln1_gain[None],
            ln1_bias[None],
            qv_bias,
            out_bias[None],
            ln2_gain[None],
            ln2_bias[None],
            down_bias[None],
        ],
        axis=0,
    )
    vectors = lax.all_gather(vectors, "dp", axis=0).transpose(1, 0, 2).reshape(8, D)
    gain_one, shift_one, bias_q, bias_v, bias_out, gain_two, shift_two, bias_down = [
        vectors[row] for row in range(8)
    ]
    qkv_full = gather(qkv_weight)
    out_full = gather(out_weight)
    up_cols = lax.all_to_all(up_weight, "dp", 1, 0, tiled=True)
    cot_low = cotangent[0]
    cot_full = cot_low.astype(F32)
    cot_all = gather(cot_low)
    dactivated = dot(cot_all, down_weight, 1, 1)

    inputs_full = tokens[0].astype(F32)
    normed_one, inverse_one, pre_one = norm_parts(inputs_full, gain_one, shift_one)
    act_one = pre_one.astype(LOW)
    mixed_qkv = dot(act_one, qkv_full, 1, 0)
    queries = (mixed_qkv[:, :D] + bias_q).astype(LOW)
    key_values = pack_pairs(mixed_qkv[:, D : 2 * D], mixed_qkv[:, 2 * D :] + bias_v).astype(LOW)
    key_values = lax.all_gather(key_values, "ctx", axis=0, tiled=True)
    attended, logs = attend(queries, key_values)
    hidden_one = inputs_full + (dot(attended, out_full, 1, 0) + bias_out)
    normed_two, inverse_two, pre_two = norm_parts(hidden_one, gain_two, shift_two)
    act_all = gather(pre_two.astype(LOW))
    pre_up = dot(act_all, up_cols, 1, 0) + up_bias
    activated = gelu_exact(pre_up).astype(LOW)
    dpre = dactivated * gelu_slope(pre_up)
    dpre_low = dpre.astype(LOW)
    dnorm_two = lax.psum_scatter(
        dot(dpre_low, up_cols, 1, 1).astype(LOW), "dp", scatter_dimension=0, tiled=True
    ).astype(F32)
    out_terms = lax.psum_scatter(
        dot(activated, down_weight, 1, 0).astype(LOW), "dp", scatter_dimension=0, tiled=True
    ).astype(F32)
    output_full = hidden_one + (out_terms + bias_down)
    down_part = dot(activated, cot_all, 0, 0).astype(LOW)
    up_part = lax.all_to_all(
        dot(act_all, dpre_low, 0, 0).astype(LOW), "dp", 0, 1, tiled=True
    )
    down_grad, up_grad = lax.psum((down_part, up_part), "ctx")

    dhidden = cot_full + norm_back(dnorm_two, normed_two, inverse_two, gain_two)
    dhidden_low = dhidden.astype(LOW)
    dattended = dot(dhidden_low, out_full, 1, 1).astype(LOW)
    out_part = dot(attended, dhidden_low, 0, 0).astype(LOW)
    dqueries, dkv, pair_sums = attend_back(queries, key_values, attended, dattended, logs)
    dkv = lax.psum_scatter(dkv, "ctx", scatter_dimension=0, tiled=True)
    dqkv = jnp.concatenate([dqueries, unpack_pairs(dkv)], axis=1)
    qkv_part = dot(act_one, dqkv, 0, 0).astype(LOW)
    dnorm_one = dot(dqkv, qkv_full, 1, 1)
    input_grad = (dhidden + norm_back(dnorm_one, normed_one, inverse_one, gain_one)).astype(LOW)
    sums = jnp.stack(
        [
            jnp.sum(dnorm_one * normed_one, axis=0),
            jnp.sum(dnorm_one, axis=0),
            pair_sums[0],
            pair_sums[1],
            jnp.sum(dhidden, axis=0),
            jnp.sum(dnorm_two * normed_two, axis=0),
            jnp.sum(dnorm_two, axis=0),
            jnp.sum(cot_full, axis=0),
        ]
    )
    sums = sums.reshape(8, shards, part).transpose(1, 0, 2).reshape(shards, 8 * part)
    sums = jnp.pad(sums.astype(LOW)[:, None], ((0, 0), (0, 15), (0, D - 8 * part)))
    columns = [qkv_part[:, :D], qkv_part[:, D : 2 * D], qkv_part[:, 2 * D :], out_part]
    packed = [column.reshape(shards, part, D) for column in columns] + [sums]
    height = 4 * part + 16
    packed = jnp.concatenate(packed, axis=1).reshape(shards * height, D)
    packed = lax.psum_scatter(packed, "dp", scatter_dimension=0, tiled=True)
    up_sums = jnp.sum(dpre, axis=0)
    packed, up_grad, down_grad = lax.optimization_barrier((packed, up_grad, down_grad))
    packed, up_bias_grad = lax.psum((packed, up_sums), "ctx")
    qkv_grad = jnp.concatenate(
        [packed[row * part : (row + 1) * part] for row in range(3)], axis=1
    ).astype(F32)
    out_grad = packed[3 * part : 4 * part].astype(F32)
    sums = packed[4 * part, : 8 * part].reshape(8, part).astype(F32)
    return (
        output_full.astype(LOW)[None],
        input_grad[None],
        sums[0],
        sums[1],
        qkv_grad,
        sums[2:4],
        out_grad,
        sums[4],
        sums[5],
        sums[6],
        up_grad.astype(F32),
        up_bias_grad,
        down_grad.astype(F32),
        sums[7],
    )


def solution(mesh):
    placed = (
        P("dp", "ctx", None),
        P("dp", "ctx", None),
        P("dp"),
        P("dp"),
        P("dp", None),
        P(None, "dp"),
        P("dp", None),
        P("dp"),
        P("dp"),
        P("dp"),
        P("dp", None),
        P("dp"),
        P("dp", None),
        P("dp"),
    )
    return jax.shard_map(
        per_device,
        mesh=mesh,
        in_specs=placed,
        out_specs=(
            P("dp", "ctx", None),
            P("dp", "ctx", None),
            P("dp"),
            P("dp"),
            P("dp", None),
            P(None, "dp"),
            P("dp", None),
            P("dp"),
            P("dp"),
            P("dp"),
            P("dp", None),
            P("dp"),
            P("dp", None),
            P("dp"),
        ),
        check_vma=False,
    )
```

```python
import functools

import jax
import jax.numpy as jnp
from jax import lax
from jax.experimental import pallas as pl
from jax.experimental.pallas import tpu as pltpu
from jax.sharding import PartitionSpec as P

D = 1088
H = 17
HD = 64


EPSILON = 1e-05
ROOT_HALF = 0.7071067811865476
INV_ROOT_TAU = 0.3989422804014327

F32 = jnp.float32
LOW = jnp.bfloat16

def norm_parts(values, norm_gain, norm_shift):
    average = jnp.mean(values, axis=-1, keepdims=True)
    centered = values - average
    inverse = lax.rsqrt(jnp.mean(centered * centered, axis=-1, keepdims=True) + EPSILON)
    normed = centered * inverse
    return (normed, inverse, normed * norm_gain + norm_shift)


def norm_back(grad_out, normed, inverse, norm_gain):
    scaled = grad_out * norm_gain
    return inverse * (
        scaled
        - jnp.mean(scaled, axis=-1, keepdims=True)
        - normed * jnp.mean(scaled * normed, axis=-1, keepdims=True)
    )


def gelu_exact(pre_act):
    return 0.5 * pre_act * (1.0 + lax.erf(pre_act * ROOT_HALF))


def gelu_slope(pre_act):
    return (
        0.5 * (1.0 + lax.erf(pre_act * ROOT_HALF))
        + pre_act * jnp.exp(-0.5 * pre_act * pre_act) * INV_ROOT_TAU
    )


def dot(left, right, left_dim, right_dim):
    return lax.dot_general(
        left, right, (((left_dim,), (right_dim,)), ((), ())), preferred_element_type=F32
    )


def gather(block):
    return lax.all_gather(block, "dp", axis=0, tiled=True)


def spread(block, axis_name):
    return lax.all_to_all(block, axis_name, 0, 0, tiled=True)


def sum_blocks(partial, shards):
    low = partial.astype(LOW).reshape(shards, partial.shape[0] // shards, partial.shape[1])
    return jnp.sum(spread(low, "dp").astype(F32), axis=0)


def to_heads(arrays, parts, width):
    padded = [jnp.pad(array, ((0, 0), (0, parts * width - D))) for array in arrays]
    blocks = [
        jnp.concatenate([array[:, i * width : (i + 1) * width] for array in padded], axis=1)
        for i in range(parts)
    ]
    received = spread(jnp.stack(blocks), "ctx")
    return received.reshape(-1, len(arrays) * width)


def to_rows(stacked, parts, width):
    received = spread(stacked.reshape(parts, -1, stacked.shape[1]), "ctx")
    return [
        jnp.concatenate(
            [received[i, :, first : first + width] for i in range(parts)], axis=1
        )[:, :D]
        for first in range(0, stacked.shape[1], width)
    ]


def allowed_pairs(first, rows, columns):
    query_pos = first + lax.broadcasted_iota(jnp.int32, (rows, columns), 0)
    return lax.broadcasted_iota(jnp.int32, (rows, columns), 1) <= query_pos


def attend_kernel(width, rows, qkv_ref, out_ref, log_ref):
    length = qkv_ref.shape[0]
    scale = float(HD) ** (-0.5)
    lane = lax.broadcasted_iota(jnp.int32, (rows, 128), 1)

    def step(block, carry):
        first = pl.multiple_of(block * rows, rows)
        own = pl.ds(first, rows)
        allowed = allowed_pairs(first, rows, length)
        logs = jnp.zeros((rows, 128), F32)
        mixed = []
        for head in range(width // HD):
            cols = slice(head * HD, (head + 1) * HD)
            key = qkv_ref[:, width + head * HD : width + (head + 1) * HD]
            value = qkv_ref[:, 2 * width + head * HD : 2 * width + (head + 1) * HD]
            scores = jnp.where(allowed, dot(qkv_ref[own, cols], key, 1, 1) * scale, -1e30)
            highest = jnp.max(scores, axis=1, keepdims=True)
            powers = jnp.exp(scores - highest)
            summed = jnp.sum(powers, axis=1, keepdims=True)
            probs_low = (powers * (1.0 / summed)).astype(LOW)
            mixed.append(dot(probs_low, value, 1, 0).astype(LOW))
            logs = jnp.where(lane == head, highest + jnp.log(summed), logs)
        out_ref[own, :] = jnp.concatenate(mixed, axis=1)
        log_ref[own, :] = logs
        return carry

    lax.fori_loop(0, length // rows, step, 0)


def attend_back_kernel(
    width, rows, qkv_ref, out_ref, dout_ref, log_ref, dqkv_ref, sum_ref, key_acc, value_acc
):
    length = qkv_ref.shape[0]
    scale = float(HD) ** (-0.5)
    key_acc[...] = jnp.zeros_like(key_acc)
    value_acc[...] = jnp.zeros_like(value_acc)
    sum_ref[...] = jnp.zeros_like(sum_ref)

    def step(block, carry):
        first = pl.multiple_of(block * rows, rows)
        own = pl.ds(first, rows)
        allowed = allowed_pairs(first, rows, length)
        for head in range(width // HD):
            cols = slice(head * HD, (head + 1) * HD)
            query = qkv_ref[own, cols]
            key = qkv_ref[:, width + head * HD : width + (head + 1) * HD]
            value = qkv_ref[:, 2 * width + head * HD : 2 * width + (head + 1) * HD]
            dout = dout_ref[own, cols]
            scores = jnp.where(allowed, dot(query, key, 1, 1) * scale, -1e30)
            probs = jnp.exp(scores - log_ref[own, head : head + 1])
            delta = jnp.sum(
                dout.astype(F32) * out_ref[own, cols].astype(F32), axis=1, keepdims=True
            )
            dscores = (probs * (dot(dout, value, 1, 1) - delta)).astype(LOW)
            dquery = dot(dscores, key, 1, 0) * scale
            dqkv_ref[own, cols] = dquery.astype(LOW)
            sum_ref[0:1, cols] += jnp.sum(dquery, axis=0, keepdims=True)
            key_acc[:, cols] += dot(dscores, query, 0, 0) * scale
            value_acc[:, cols] += dot(probs.astype(LOW), dout, 0, 0)
        return carry

    lax.fori_loop(0, length // rows, step, 0)
    dqkv_ref[:, width : 2 * width] = key_acc[...].astype(LOW)
    dqkv_ref[:, 2 * width :] = value_acc[...].astype(LOW)
    sum_ref[1:2, :] = jnp.sum(value_acc[...], axis=0, keepdims=True)


def attend(qkv, width, rows):
    length = qkv.shape[0]
    return pl.pallas_call(
        functools.partial(attend_kernel, width, rows),
        out_shape=(
            jax.ShapeDtypeStruct((length, width), LOW),
            jax.ShapeDtypeStruct((length, 128), F32),
        ),
        cost_estimate=pl.CostEstimate(
            flops=4 * length * length * width,
            bytes_accessed=8 * length * width,
            transcendentals=length * length * width // HD,
        ),
        name="attend",
    )(qkv)


def attend_back(qkv, attended, dattended, logs, width, rows):
    length = qkv.shape[0]
    return pl.pallas_call(
        functools.partial(attend_back_kernel, width, rows),
        out_shape=(
            jax.ShapeDtypeStruct((length, 3 * width), LOW),
            jax.ShapeDtypeStruct((2, width), F32),
        ),
        scratch_shapes=[pltpu.VMEM((length, width), F32), pltpu.VMEM((length, width), F32)],
        cost_estimate=pl.CostEstimate(
            flops=10 * length * length * width,
            bytes_accessed=16 * length * width,
            transcendentals=length * length * width // HD,
        ),
        name="attend_back",
    )(qkv, attended, dattended, logs)


def per_device(
    tokens,
    cotangent,
    ln1_gain,
    ln1_bias,
    qkv_weight,
    qv_bias,
    out_weight,
    out_bias,
    ln2_gain,
    ln2_bias,
    up_weight,
    up_bias,
    down_weight,
    down_bias,
):
    shards = lax.axis_size("dp")
    part = D // shards
    vectors = jnp.concatenate(
        [
            ln1_gain[None],
            ln1_bias[None],
            qv_bias,
            out_bias[None],
            ln2_gain[None],
            ln2_bias[None],
            down_bias[None],
        ],
        axis=0,
    )
    vectors = lax.all_gather(vectors, "dp", axis=0).transpose(1, 0, 2).reshape(8, D)
    gain_one, shift_one, bias_q, bias_v, bias_out, gain_two, shift_two, bias_down = [
        vectors[row] for row in range(8)
    ]
    parts = lax.axis_size("ctx")
    width = -(-H // parts) * HD
    local_count = tokens.shape[1]
    qkv_full = gather(qkv_weight)
    up_cols = lax.all_to_all(up_weight, "dp", 1, 0, tiled=True)
    cot_low = cotangent[0]
    cot_full = cot_low.astype(F32)
    qkv_full, out_low, cot_low = lax.optimization_barrier((qkv_full, out_weight, cot_low))
    out_full = gather(out_low)
    out_full, cot_low = lax.optimization_barrier((out_full, cot_low))
    cot_all = gather(cot_low)
    dactivated = dot(cot_all, down_weight, 1, 1)

    inputs_full = tokens[0].astype(F32)
    normed_one, inverse_one, pre_one = norm_parts(inputs_full, gain_one, shift_one)
    act_one = pre_one.astype(LOW)
    mixed_qkv = dot(act_one, qkv_full, 1, 0)
    head_qkv = to_heads(
        [
            (mixed_qkv[:, :D] + bias_q).astype(LOW),
            mixed_qkv[:, D : 2 * D].astype(LOW),
            (mixed_qkv[:, 2 * D :] + bias_v).astype(LOW),
        ],
        parts,
        width,
    )
    head_out, logs = attend(head_qkv, width, local_count)
    (attended,) = to_rows(head_out, parts, width)
    hidden_one = inputs_full + (dot(attended, out_full, 1, 0) + bias_out)
    normed_two, inverse_two, pre_two = norm_parts(hidden_one, gain_two, shift_two)
    act_two, cot_all, up_cols = lax.optimization_barrier(
        (pre_two.astype(LOW), cot_all, up_cols)
    )
    act_all = gather(act_two)
    act_all, act_one_late = lax.optimization_barrier((act_all, act_one))
    act_one_all = gather(act_one_late)
    pre_up = dot(act_all, up_cols, 1, 0) + up_bias
    activated = gelu_exact(pre_up).astype(LOW)
    dpre = dactivated * gelu_slope(pre_up)
    dpre_low = dpre.astype(LOW)
    dnorm_two = sum_blocks(dot(dpre_low, up_cols, 1, 1), shards)
    dnorm_two, activated = lax.optimization_barrier((dnorm_two, activated))
    down_part = dot(activated, cot_all, 0, 0).astype(LOW)
    up_part = lax.all_to_all(
        dot(act_all, dpre_low, 0, 0).astype(LOW), "dp", 0, 1, tiled=True
    )
    down_grad, up_grad = lax.psum((down_part, up_part), "ctx")

    dhidden = cot_full + norm_back(dnorm_two, normed_two, inverse_two, gain_two)
    dhidden_low = dhidden.astype(LOW)
    dattended = dot(dhidden_low, out_full, 1, 1).astype(LOW)
    out_grad = lax.psum_scatter(
        dot(attended, dhidden_low, 0, 0).astype(LOW), "dp", scatter_dimension=0, tiled=True
    )
    head_dout = to_heads([dattended], parts, width)
    head_dqkv, head_sums = attend_back(head_qkv, head_out, head_dout, logs, width, local_count)
    dqkv = jnp.concatenate(to_rows(head_dqkv, parts, width), axis=1)
    pair_sums = lax.dynamic_update_slice(
        jnp.zeros((2, parts * width), F32), head_sums, (0, lax.axis_index("ctx") * width)
    )[:, :D]
    dqkv_all = lax.all_to_all(dqkv, "dp", 1, 0, tiled=True)
    qkv_part = dot(act_one_all, dqkv_all, 0, 0).astype(LOW)
    dnorm_one = dot(dqkv, qkv_full, 1, 1)
    input_grad = (dhidden + norm_back(dnorm_one, normed_one, inverse_one, gain_one)).astype(LOW)
    sums = jnp.stack(
        [
            jnp.sum(dnorm_one * normed_one, axis=0),
            jnp.sum(dnorm_one, axis=0),
            pair_sums[0],
            pair_sums[1],
            jnp.sum(dhidden, axis=0),
            jnp.sum(dnorm_two * normed_two, axis=0),
            jnp.sum(dnorm_two, axis=0),
            jnp.sum(cot_full, axis=0),
        ]
    )
    sums = sums.reshape(8, shards, part).transpose(1, 0, 2).reshape(shards, 8 * part)
    columns = 3 * part
    sums = jnp.pad(sums.astype(LOW), ((0, 0), (0, part))).reshape(shards, 3, columns)
    spare = -(part + 3) % 16
    packed = jnp.concatenate(
        [qkv_part.reshape(shards, part, columns), jnp.pad(sums, ((0, 0), (0, spare), (0, 0)))],
        axis=1,
    )
    packed = spread(packed, "dp")
    qkv_mine = packed[:, :part].transpose(1, 0, 2).reshape(part, 3 * D)
    sums_mine = jnp.sum(
        packed[:, part : part + 3].astype(F32).reshape(shards, 9 * part)[:, : 8 * part], axis=0
    )
    qkv_mine, activated = lax.optimization_barrier((qkv_mine, activated))
    output_full = hidden_one + (sum_blocks(dot(activated, down_weight, 1, 0), shards) + bias_down)
    small = jnp.concatenate([sums_mine, jnp.sum(dpre, axis=0)])
    qkv_mine, up_grad, down_grad, small, out_grad = lax.optimization_barrier(
        (qkv_mine, up_grad, down_grad, small, out_grad)
    )
    qkv_grad, out_grad, small = lax.psum((qkv_mine, out_grad, small), "ctx")
    qkv_grad = qkv_grad.astype(F32)
    out_grad = out_grad.astype(F32)
    sums = small[: 8 * part].reshape(8, part)
    up_bias_grad = small[8 * part :]
    return (
        output_full.astype(LOW)[None],
        input_grad[None],
        sums[0],
        sums[1],
        qkv_grad,
        sums[2:4],
        out_grad,
        sums[4],
        sums[5],
        sums[6],
        up_grad.astype(F32),
        up_bias_grad,
        down_grad.astype(F32),
        sums[7],
    )


def solution(mesh):
    placed = (
        P("dp", "ctx", None),
        P("dp", "ctx", None),
        P("dp"),
        P("dp"),
        P("dp", None),
        P(None, "dp"),
        P("dp", None),
        P("dp"),
        P("dp"),
        P("dp"),
        P("dp", None),
        P("dp"),
        P("dp", None),
        P("dp"),
    )
    return jax.shard_map(
        per_device,
        mesh=mesh,
        in_specs=placed,
        out_specs=(
            P("dp", "ctx", None),
            P("dp", "ctx", None),
            P("dp"),
            P("dp"),
            P("dp", None),
            P(None, "dp"),
            P("dp", None),
            P("dp"),
            P("dp"),
            P("dp"),
            P("dp", None),
            P("dp"),
            P("dp", None),
            P("dp"),
        ),
        check_vma=False,
    )
```

```python
import functools

import jax
import jax.numpy as jnp
from jax import lax
from jax.experimental import pallas as pl
from jax.experimental.pallas import tpu as pltpu
from jax.sharding import PartitionSpec as P

D = 1088
H = 17
HD = 64


EPSILON = 1e-05
ROOT_HALF = 0.7071067811865476
INV_ROOT_TAU = 0.3989422804014327

F32 = jnp.float32
LOW = jnp.bfloat16

def norm_parts(values, norm_gain, norm_shift):
    average = jnp.mean(values, axis=-1, keepdims=True)
    centered = values - average
    inverse = lax.rsqrt(jnp.mean(centered * centered, axis=-1, keepdims=True) + EPSILON)
    normed = centered * inverse
    return (normed, inverse, normed * norm_gain + norm_shift)


def norm_back(grad_out, normed, inverse, norm_gain):
    scaled = grad_out * norm_gain
    return inverse * (
        scaled
        - jnp.mean(scaled, axis=-1, keepdims=True)
        - normed * jnp.mean(scaled * normed, axis=-1, keepdims=True)
    )


def gelu_exact(pre_act):
    return 0.5 * pre_act * (1.0 + lax.erf(pre_act * ROOT_HALF))


def gelu_slope(pre_act):
    return (
        0.5 * (1.0 + lax.erf(pre_act * ROOT_HALF))
        + pre_act * jnp.exp(-0.5 * pre_act * pre_act) * INV_ROOT_TAU
    )


def dot(left, right, left_dim, right_dim):
    return lax.dot_general(
        left, right, (((left_dim,), (right_dim,)), ((), ())), preferred_element_type=F32
    )


def gather(block):
    return lax.all_gather(block, "dp", axis=0, tiled=True)


def spread(block, axis_name):
    return lax.all_to_all(block, axis_name, 0, 0, tiled=True)


def sum_blocks(partial, shards):
    low = partial.astype(LOW).reshape(shards, partial.shape[0] // shards, partial.shape[1])
    return jnp.sum(spread(low, "dp").astype(F32), axis=0)


def to_heads(arrays, parts, width):
    padded = [jnp.pad(array, ((0, 0), (0, parts * width - D))) for array in arrays]
    blocks = [
        jnp.concatenate([array[:, i * width : (i + 1) * width] for array in padded], axis=1)
        for i in range(parts)
    ]
    received = spread(jnp.stack(blocks), "ctx")
    return received.reshape(-1, len(arrays) * width)


def to_rows(stacked, parts, width):
    received = spread(stacked.reshape(parts, -1, stacked.shape[1]), "ctx")
    return [
        jnp.concatenate(
            [received[i, :, first : first + width] for i in range(parts)], axis=1
        )[:, :D]
        for first in range(0, stacked.shape[1], width)
    ]


def allowed_pairs(first, rows, columns):
    query_pos = first + lax.broadcasted_iota(jnp.int32, (rows, columns), 0)
    return lax.broadcasted_iota(jnp.int32, (rows, columns), 1) <= query_pos


def attend_kernel(width, rows, qkv_ref, out_ref, log_ref):
    length = qkv_ref.shape[0]
    scale = float(HD) ** (-0.5)
    lane = lax.broadcasted_iota(jnp.int32, (rows, 128), 1)

    def step(block, carry):
        first = pl.multiple_of(block * rows, rows)
        own = pl.ds(first, rows)
        allowed = allowed_pairs(first, rows, length)
        logs = jnp.zeros((rows, 128), F32)
        mixed = []
        for head in range(width // HD):
            cols = slice(head * HD, (head + 1) * HD)
            key = qkv_ref[:, width + head * HD : width + (head + 1) * HD]
            value = qkv_ref[:, 2 * width + head * HD : 2 * width + (head + 1) * HD]
            scores = jnp.where(allowed, dot(qkv_ref[own, cols], key, 1, 1) * scale, -1e30)
            highest = jnp.max(scores, axis=1, keepdims=True)
            powers = jnp.exp(scores - highest)
            summed = jnp.sum(powers, axis=1, keepdims=True)
            probs_low = (powers * (1.0 / summed)).astype(LOW)
            mixed.append(dot(probs_low, value, 1, 0).astype(LOW))
            logs = jnp.where(lane == head, highest + jnp.log(summed), logs)
        out_ref[own, :] = jnp.concatenate(mixed, axis=1)
        log_ref[own, :] = logs
        return carry

    lax.fori_loop(0, length // rows, step, 0)


def attend_back_kernel(
    width, rows, qkv_ref, out_ref, dout_ref, log_ref, dqkv_ref, sum_ref, key_acc, value_acc
):
    length = qkv_ref.shape[0]
    scale = float(HD) ** (-0.5)
    key_acc[...] = jnp.zeros_like(key_acc)
    value_acc[...] = jnp.zeros_like(value_acc)
    sum_ref[...] = jnp.zeros_like(sum_ref)

    def step(block, carry):
        first = pl.multiple_of(block * rows, rows)
        own = pl.ds(first, rows)
        allowed = allowed_pairs(first, rows, length)
        for head in range(width // HD):
            cols = slice(head * HD, (head + 1) * HD)
            query = qkv_ref[own, cols]
            key = qkv_ref[:, width + head * HD : width + (head + 1) * HD]
            value = qkv_ref[:, 2 * width + head * HD : 2 * width + (head + 1) * HD]
            dout = dout_ref[own, cols]
            scores = jnp.where(allowed, dot(query, key, 1, 1) * scale, -1e30)
            probs = jnp.exp(scores - log_ref[own, head : head + 1])
            delta = jnp.sum(
                dout.astype(F32) * out_ref[own, cols].astype(F32), axis=1, keepdims=True
            )
            dscores = (probs * (dot(dout, value, 1, 1) - delta)).astype(LOW)
            dquery = dot(dscores, key, 1, 0) * scale
            dqkv_ref[own, cols] = dquery.astype(LOW)
            sum_ref[0:1, cols] += jnp.sum(dquery, axis=0, keepdims=True)
            key_acc[:, cols] += dot(dscores, query, 0, 0) * scale
            value_acc[:, cols] += dot(probs.astype(LOW), dout, 0, 0)
        return carry

    lax.fori_loop(0, length // rows, step, 0)
    dqkv_ref[:, width : 2 * width] = key_acc[...].astype(LOW)
    dqkv_ref[:, 2 * width :] = value_acc[...].astype(LOW)
    sum_ref[1:2, :] = jnp.sum(value_acc[...], axis=0, keepdims=True)


def attend(qkv, width, rows):
    length = qkv.shape[0]
    return pl.pallas_call(
        functools.partial(attend_kernel, width, rows),
        out_shape=(
            jax.ShapeDtypeStruct((length, width), LOW),
            jax.ShapeDtypeStruct((length, 128), F32),
        ),
        cost_estimate=pl.CostEstimate(
            flops=4 * length * length * width,
            bytes_accessed=8 * length * width,
            transcendentals=length * length * width // HD,
        ),
        name="attend",
    )(qkv)


def attend_back(qkv, attended, dattended, logs, width, rows):
    length = qkv.shape[0]
    return pl.pallas_call(
        functools.partial(attend_back_kernel, width, rows),
        out_shape=(
            jax.ShapeDtypeStruct((length, 3 * width), LOW),
            jax.ShapeDtypeStruct((2, width), F32),
        ),
        scratch_shapes=[pltpu.VMEM((length, width), F32), pltpu.VMEM((length, width), F32)],
        cost_estimate=pl.CostEstimate(
            flops=10 * length * length * width,
            bytes_accessed=16 * length * width,
            transcendentals=length * length * width // HD,
        ),
        name="attend_back",
    )(qkv, attended, dattended, logs)


def per_device(
    tokens,
    cotangent,
    ln1_gain,
    ln1_bias,
    qkv_weight,
    qv_bias,
    out_weight,
    out_bias,
    ln2_gain,
    ln2_bias,
    up_weight,
    up_bias,
    down_weight,
    down_bias,
):
    shards = lax.axis_size("dp")
    part = D // shards
    vectors = jnp.concatenate(
        [
            ln1_gain[None],
            ln1_bias[None],
            qv_bias,
            out_bias[None],
            ln2_gain[None],
            ln2_bias[None],
            down_bias[None],
        ],
        axis=0,
    )
    vectors = lax.all_gather(vectors, "dp", axis=0).transpose(1, 0, 2).reshape(8, D)
    gain_one, shift_one, bias_q, bias_v, bias_out, gain_two, shift_two, bias_down = [
        vectors[row] for row in range(8)
    ]
    parts = lax.axis_size("ctx")
    width = -(-H // parts) * HD
    local_count = tokens.shape[1]
    qkv_full = gather(qkv_weight)
    up_cols = lax.all_to_all(up_weight, "dp", 1, 0, tiled=True)
    cot_low = cotangent[0]
    cot_full = cot_low.astype(F32)
    inputs_full = tokens[0].astype(F32)
    normed_one, inverse_one, pre_one = norm_parts(inputs_full, gain_one, shift_one)
    act_one = pre_one.astype(LOW)
    act_one, out_low = lax.optimization_barrier((act_one, out_weight))
    out_full = gather(out_low)
    mixed_qkv = dot(act_one, qkv_full, 1, 0)
    mixed_qkv, cot_low = lax.optimization_barrier((mixed_qkv, cot_low))
    cot_all = gather(cot_low)
    dactivated = dot(cot_all, down_weight, 1, 1)
    head_qkv = to_heads(
        [
            (mixed_qkv[:, :D] + bias_q).astype(LOW),
            mixed_qkv[:, D : 2 * D].astype(LOW),
            (mixed_qkv[:, 2 * D :] + bias_v).astype(LOW),
        ],
        parts,
        width,
    )
    head_qkv, act_one_late = lax.optimization_barrier((head_qkv, act_one))
    act_one_all = gather(act_one_late)
    head_out, logs = attend(head_qkv, width, local_count)
    head_out, up_cols = lax.optimization_barrier((head_out, up_cols))
    (attended,) = to_rows(head_out, parts, width)
    hidden_one = inputs_full + (dot(attended, out_full, 1, 0) + bias_out)
    normed_two, inverse_two, pre_two = norm_parts(hidden_one, gain_two, shift_two)
    act_two, dactivated, act_one_all = lax.optimization_barrier(
        (pre_two.astype(LOW), dactivated, act_one_all)
    )
    act_all = gather(act_two)
    pre_up = dot(act_all, up_cols, 1, 0) + up_bias
    activated = gelu_exact(pre_up).astype(LOW)
    dpre = dactivated * gelu_slope(pre_up)
    dpre_low = dpre.astype(LOW)
    dnorm_two = sum_blocks(dot(dpre_low, up_cols, 1, 1), shards)
    dnorm_two, activated, act_late, dpre_late = lax.optimization_barrier(
        (dnorm_two, activated, act_all, dpre_low)
    )
    down_part = dot(activated, cot_all, 0, 0).astype(LOW)
    up_part = lax.all_to_all(
        dot(act_late, dpre_late, 0, 0).astype(LOW), "dp", 0, 1, tiled=True
    )
    dhidden = cot_full + norm_back(dnorm_two, normed_two, inverse_two, gain_two)
    dhidden_low = dhidden.astype(LOW)
    dattended = dot(dhidden_low, out_full, 1, 1).astype(LOW)
    out_grad = sum_blocks(dot(attended, dhidden_low, 0, 0), shards).astype(LOW)
    head_dout = to_heads([dattended], parts, width)
    head_dout, up_part, down_part = lax.optimization_barrier((head_dout, up_part, down_part))
    down_grad, up_grad = lax.psum((down_part, up_part), "ctx")
    head_dqkv, head_sums = attend_back(head_qkv, head_out, head_dout, logs, width, local_count)
    dqkv = jnp.concatenate(to_rows(head_dqkv, parts, width), axis=1)
    pair_sums = lax.dynamic_update_slice(
        jnp.zeros((2, parts * width), F32), head_sums, (0, lax.axis_index("ctx") * width)
    )[:, :D]
    dqkv_all = lax.all_to_all(dqkv, "dp", 1, 0, tiled=True)
    qkv_part = dot(act_one_all, dqkv_all, 0, 0).astype(LOW)
    dnorm_one = dot(dqkv, qkv_full, 1, 1)
    input_grad = (dhidden + norm_back(dnorm_one, normed_one, inverse_one, gain_one)).astype(LOW)
    sums = jnp.stack(
        [
            jnp.sum(dnorm_one * normed_one, axis=0),
            jnp.sum(dnorm_one, axis=0),
            pair_sums[0],
            pair_sums[1],
            jnp.sum(dhidden, axis=0),
            jnp.sum(dnorm_two * normed_two, axis=0),
            jnp.sum(dnorm_two, axis=0),
            jnp.sum(cot_full, axis=0),
        ]
    )
    sums = sums.reshape(8, shards, part).transpose(1, 0, 2).reshape(shards, 8 * part)
    columns = 3 * part
    sums = jnp.pad(sums.astype(LOW), ((0, 0), (0, part))).reshape(shards, 3, columns)
    spare = -(part + 3) % 16
    packed = jnp.concatenate(
        [qkv_part.reshape(shards, part, columns), jnp.pad(sums, ((0, 0), (0, spare), (0, 0)))],
        axis=1,
    )
    packed = spread(packed, "dp")
    qkv_mine = packed[:, :part].transpose(1, 0, 2).reshape(part, 3 * D)
    sums_mine = jnp.sum(
        packed[:, part : part + 3].astype(F32).reshape(shards, 9 * part)[:, : 8 * part], axis=0
    )
    qkv_mine, activated = lax.optimization_barrier((qkv_mine, activated))
    output_full = hidden_one + (sum_blocks(dot(activated, down_weight, 1, 0), shards) + bias_down)
    small = jnp.concatenate([sums_mine, jnp.sum(dpre, axis=0)])
    qkv_mine, up_grad, down_grad, small, out_grad = lax.optimization_barrier(
        (qkv_mine, up_grad, down_grad, small, out_grad)
    )
    qkv_grad, out_grad, small = lax.psum((qkv_mine, out_grad, small), "ctx")
    qkv_grad = qkv_grad.astype(F32)
    out_grad = out_grad.astype(F32)
    sums = small[: 8 * part].reshape(8, part)
    up_bias_grad = small[8 * part :]
    return (
        output_full.astype(LOW)[None],
        input_grad[None],
        sums[0],
        sums[1],
        qkv_grad,
        sums[2:4],
        out_grad,
        sums[4],
        sums[5],
        sums[6],
        up_grad.astype(F32),
        up_bias_grad,
        down_grad.astype(F32),
        sums[7],
    )


def solution(mesh):
    placed = (
        P("dp", "ctx", None),
        P("dp", "ctx", None),
        P("dp"),
        P("dp"),
        P("dp", None),
        P(None, "dp"),
        P("dp", None),
        P("dp"),
        P("dp"),
        P("dp"),
        P("dp", None),
        P("dp"),
        P("dp", None),
        P("dp"),
    )
    return jax.shard_map(
        per_device,
        mesh=mesh,
        in_specs=placed,
        out_specs=(
            P("dp", "ctx", None),
            P("dp", "ctx", None),
            P("dp"),
            P("dp"),
            P("dp", None),
            P(None, "dp"),
            P("dp", None),
            P("dp"),
            P("dp"),
            P("dp"),
            P("dp", None),
            P("dp"),
            P("dp", None),
            P("dp"),
        ),
        check_vma=False,
    )
```
